128 devices in a mesh: fronts: 8 (over y, core), rows: 16 (over z, x).
Axes of the slice: x: 4, y: 4, z: 4, core: 2. Of those that a mesh axis runs over, the one named last changes fastest.
Arguments:
- lower_rhs: float32 [16, 16384, 512], P('fronts', 'rows'), may hold values from -6 to 6
- lower_vectors: float32 [16, 16384, 256], P('fronts', 'rows')
- lower_factors: float32 [16, 16, 256, 256], P('fronts', 'rows')
- merge_vectors: float32 [16, 16, 256, 256], P('fronts', 'rows')
- merge_factors: float32 [16, 16, 256, 256], P('fronts', 'rows')
- live_blocks: int32 [16], replicated, may hold values from 1 to 16, 128 in all
- parent_front: int32 [16, 1], replicated, may hold values from 0 to 7, as said below
- front_owner: int32 [8], replicated, may hold values from 0 to 7, as said below
- contrib_rows: int32 [16, 128], replicated, may hold values from 0 to 16383, as said below
- upper_rhs: float32 [8, 16384, 512], P('fronts', 'rows'), may hold values from -6 to 6
- upper_vectors: float32 [8, 16384, 256], P('fronts', 'rows')
- upper_factors: float32 [8, 16, 256, 256], P('fronts', 'rows')
- summit_vectors: float32 [8, 16, 256, 256], P('fronts', 'rows')
- summit_factors: float32 [8, 16, 256, 256], P('fronts', 'rows')
Outputs:
- lower_result: float32 [16, 16384, 512], P('fronts', 'rows')
- upper_result: float32 [8, 16384, 512], P('fronts', 'rows')
The draws below stay inside these ranges and needn't reach their ends.
Inputs may be any that keep to these rules, and one draw needn't show every extreme that they name: `parent_front`: every parent front has between one and 4 children, and some parent has exactly 4. `front_owner`: each parent front has its own index of fronts. `contrib_rows`: row k of a child's contribution lands in its parent's row block k // 8; no two entries are equal.
All inputs are finite; a program needn't handle non-finite values.
Results may differ from the reference program's by a relative error of at most 0.0003.
Values sent between devices are 32-bit elements; how exact they have to be, the bound alone decides.
No kernel may reach another device: no remote copies, remote signals or barrier semaphores. Data moves between devices by JAX's collectives and lax.ppermute only.
A program may use at most 128 MiB of HBM per device.

```python
import math
import jax
import jax.numpy as jnp
import numpy as np
from jax import lax

N = 512
BR = 1024
K = 256
NPIV = 128
FR1 = 2
MAXCH = 4
CB = 128
CONTRIB_PER_BLOCK = 8
LOWER_FRONTS = 16
F2 = 8
FROWS = 16384
LEVELS = 4
N_ROWS = 16


def compact_factor(vectors):
    gram_matrix = jnp.einsum('cri,crj->cij', vectors, vectors, precision=lax.Precision.HIGHEST)
    unit_matrix = jnp.eye(gram_matrix.shape[-1], dtype=jnp.float32)
    triangle = jnp.triu(gram_matrix, 1) + 0.5 * gram_matrix * unit_matrix
    identity_stack = jnp.broadcast_to(unit_matrix, gram_matrix.shape)
    return jax.scipy.linalg.solve_triangular(triangle, identity_stack, lower=False)


def block_reflectors(key, number):
    normal = jax.random.normal(key, (number, BR, K), jnp.float32)
    spread = 1.0 / BR ** 0.5
    row_index = lax.broadcasted_iota(jnp.int32, (BR, K), 0)
    column_index = lax.broadcasted_iota(jnp.int32, (BR, K), 1)
    vectors = jnp.where(row_index > column_index, spread * normal, jnp.where(row_index == column_index, 1.0, 0.0))
    return (vectors, compact_factor(vectors))


def node_reflectors(key, number):
    normal = jax.random.normal(key, (number, K, K), jnp.float32)
    spread = (2.0 / K) ** 0.5
    upper_part = jnp.triu(spread * normal)
    unit_stack = jnp.broadcast_to(jnp.eye(K, dtype=jnp.float32), upper_part.shape)
    return (upper_part, compact_factor(jnp.concatenate([unit_stack, upper_part], axis=1)))


def draw_lower_vectors(key, part):
    vectors, factors = block_reflectors(jax.random.fold_in(key, 11), LOWER_FRONTS * N_ROWS)
    return vectors.reshape(LOWER_FRONTS, FROWS, K)


def draw_lower_factors(key, part):
    vectors, factors = block_reflectors(jax.random.fold_in(key, 11), LOWER_FRONTS * N_ROWS)
    return factors.reshape(LOWER_FRONTS, N_ROWS, K, K)


def draw_merge_vectors(key, part):
    vectors, factors = node_reflectors(jax.random.fold_in(key, 12), LOWER_FRONTS * N_ROWS)
    return vectors.reshape(LOWER_FRONTS, N_ROWS, K, K)


def draw_merge_factors(key, part):
    vectors, factors = node_reflectors(jax.random.fold_in(key, 12), LOWER_FRONTS * N_ROWS)
    return factors.reshape(LOWER_FRONTS, N_ROWS, K, K)


def draw_upper_vectors(key, part):
    vectors, factors = block_reflectors(jax.random.fold_in(key, 13), F2 * N_ROWS)
    return vectors.reshape(F2, FROWS, K)


def draw_upper_factors(key, part):
    vectors, factors = block_reflectors(jax.random.fold_in(key, 13), F2 * N_ROWS)
    return factors.reshape(F2, N_ROWS, K, K)


def draw_summit_vectors(key, part):
    vectors, factors = node_reflectors(jax.random.fold_in(key, 14), F2 * N_ROWS)
    return vectors.reshape(F2, N_ROWS, K, K)


def draw_summit_factors(key, part):
    vectors, factors = node_reflectors(jax.random.fold_in(key, 14), F2 * N_ROWS)
    return factors.reshape(F2, N_ROWS, K, K)


def ownership(key):
    base_key = jax.random.fold_in(key, 21)
    held = jax.random.permutation(jax.random.fold_in(base_key, 1), F2).astype(jnp.int32)
    owner = jnp.argsort(held).astype(jnp.int32)
    shuffled = jax.random.permutation(jax.random.fold_in(base_key, 2), F2).astype(jnp.int32)
    child_index = jnp.arange(LOWER_FRONTS, dtype=jnp.int32)
    device = child_index // FR1
    slot_index = child_index % FR1
    next_parent = held[(device + F2 // 2) % F2]
    picked = jnp.clip(device - (MAXCH - 2), 0, F2 - 1)
    crowd_parent = jnp.where(device < MAXCH - 1, shuffled[0], shuffled[picked])
    parent = jnp.where(slot_index == FR1 - 1, next_parent, crowd_parent)
    return (parent.astype(jnp.int32), owner)


def draw_parent_front(key, part):
    parent, owner = ownership(key)
    return parent.reshape(LOWER_FRONTS, 1)


def draw_front_owner(key, part):
    parent, owner = ownership(key)
    return owner


def block_offsets(key):
    selected_count = LOWER_FRONTS * CONTRIB_PER_BLOCK
    others = jax.random.permutation(jax.random.fold_in(key, 1), BR - 2)[:selected_count - 2] + 1
    chosen = jnp.concatenate([jnp.array([0, BR - 1], jnp.int32), others.astype(jnp.int32)])
    return jax.random.permutation(jax.random.fold_in(key, 2), chosen)


def draw_contrib_rows(key, part):
    block_keys = jax.random.split(jax.random.fold_in(key, 15), N_ROWS)
    row_offsets = jax.vmap(block_offsets)(block_keys)
    begin_positions = (jnp.arange(N_ROWS, dtype=jnp.int32) * BR)[:, None]
    positioned_rows = (row_offsets + begin_positions).reshape(N_ROWS, LOWER_FRONTS, CONTRIB_PER_BLOCK)
    return jnp.transpose(positioned_rows, (1, 0, 2)).reshape(LOWER_FRONTS, CB).astype(jnp.int32)


def steps_of(own_key, shape, cuts, least, top_value):
    gain = 1.0
    for position, shards_of in cuts:
        heights = jax.random.uniform(jax.random.fold_in(jax.random.fold_in(own_key, 6), position), (shards_of,), jnp.float32, least / len(cuts), top_value / len(cuts))
        gain = gain * jnp.repeat(jnp.exp(heights), shape[position] // shards_of).reshape((-1,) + (1,) * (len(shape) - 1 - position))
    return gain


def length_profile(count, total, bound, skew):
    portions = [(1 << 20) // math.isqrt(grade ** skew) + 1 for grade in range(2, count + 1)]
    spare, given = total - bound - (count - 1), [1] * (count - 1)
    while spare > 0:
        movable = [i for i in range(count - 1) if given[i] < bound]
        whole, left = sum([portions[i] for i in movable]), spare
        for i in movable:
            extra = min(bound - given[i], max(1, left * portions[i] // whole), spare)
            given[i] = given[i] + extra
            spare = spare - extra
    return np.array([bound] + given)


def uneven_parts(stream_key, count, total, reach, lean):
    if count == 2:
        one = jax.random.randint(stream_key, (), max(1, total - reach), min(reach, total - 1) + 1)
        return jnp.stack([one, total - one])
    sizes = jnp.asarray(length_profile(count, total, reach, lean), jnp.int32)
    twos = (count - 1) // 2
    giver, taker = sizes[1:1 + 2 * twos:2], sizes[2:2 + 2 * twos:2]
    slack = jnp.minimum(giver - 1, reach - taker)
    passed = jax.random.randint(jax.random.fold_in(stream_key, 1), (twos,), 0, 1 << 20) % (slack + 1)
    sizes = sizes.at[1:1 + 2 * twos:2].set(giver - passed).at[2:2 + 2 * twos:2].set(taker + passed)
    return sizes[jax.random.permutation(jax.random.fold_in(stream_key, 2), count)]


def gaussian(key, dims, scale, most, cuts=(), kind=jnp.bfloat16):
    values = scale * jax.random.normal(key, dims, jnp.float32)
    if cuts:
        values = values * steps_of(key, dims, cuts, -0.22, 0.18)
    return jnp.clip(values, -most, most).astype(kind)


def setup_inputs(seed: int = 0) -> dict:
    key_list = jax.random.split(jax.random.key(seed), 15)
    return {
        "lower_rhs": gaussian(key_list[0], (LOWER_FRONTS, FROWS, N), 1.0, 6.0, ((0, 8), (1, 16)), jnp.float32),
        "lower_vectors": draw_lower_vectors(jax.random.fold_in(key_list[14], 71), 0),
        "lower_factors": draw_lower_factors(jax.random.fold_in(key_list[14], 71), 0),
        "merge_vectors": draw_merge_vectors(jax.random.fold_in(key_list[14], 71), 0),
        "merge_factors": draw_merge_factors(jax.random.fold_in(key_list[14], 71), 0),
        "live_blocks": uneven_parts(key_list[5], LOWER_FRONTS, LOWER_FRONTS * N_ROWS // 2, N_ROWS, 2).astype(jnp.int32),
        "parent_front": draw_parent_front(jax.random.fold_in(key_list[14], 71), 0),
        "front_owner": draw_front_owner(jax.random.fold_in(key_list[14], 71), 0),
        "contrib_rows": draw_contrib_rows(jax.random.fold_in(key_list[14], 71), 0),
        "upper_rhs": gaussian(key_list[9], (F2, FROWS, N), 1.0, 6.0, ((0, 8), (1, 16)), jnp.float32),
        "upper_vectors": draw_upper_vectors(jax.random.fold_in(key_list[14], 71), 0),
        "upper_factors": draw_upper_factors(jax.random.fold_in(key_list[14], 71), 0),
        "summit_vectors": draw_summit_vectors(jax.random.fold_in(key_list[14], 71), 0),
        "summit_factors": draw_summit_factors(jax.random.fold_in(key_list[14], 71), 0),
    }


EXACT = lax.Precision.HIGHEST

def contract(form, left, right):
    return jnp.einsum(form, left, right, precision=EXACT)

def apply_front(values, vectors, factors, pair_vectors, pair_factors, live):
    values = values.reshape(N_ROWS, BR, -1)
    vectors = vectors.reshape(N_ROWS, BR, K)
    project = contract('fri,frn->fin', vectors, values)
    scaled = contract('fij,fin->fjn', factors, project)
    applied = values - contract('fri,fin->frn', vectors, scaled)
    index = jnp.arange(N_ROWS, dtype=jnp.int32)
    applied = jnp.where((index < live)[:, None, None], applied, values)
    tops = applied[:, :K]
    for level in range(LEVELS):
        step = 2 ** level
        lead = tops[0::2 * step]
        rest = tops[step::2 * step]
        node_vec = pair_vectors[step::2 * step]
        node_fac = pair_factors[step::2 * step]
        inner = lead + contract('fij,fin->fjn', node_vec, rest)
        weight = contract('fij,fin->fjn', node_fac, inner)
        new_lead = lead - weight
        new_rest = rest - contract('fij,fjn->fin', node_vec, weight)
        active = (index[step::2 * step] < live)[:, None, None]
        tops = tops.at[0::2 * step].set(jnp.where(active, new_lead, lead))
        tops = tops.at[step::2 * step].set(jnp.where(active, new_rest, rest))
    return (tops, applied)

def reference(lower_rhs, lower_vectors, lower_factors, merge_vectors, merge_factors, live_blocks, parent_front, front_owner, contrib_rows, upper_rhs, upper_vectors, upper_factors, summit_vectors, summit_factors):

    def lower_one(operands):
        values, vectors, factors, pair_vectors, pair_factors, live = operands
        tops, applied = apply_front(values, vectors, factors, pair_vectors, pair_factors, live)
        keep = jnp.arange(K, dtype=jnp.int32) < NPIV
        root = jnp.where(keep[:, None], tops[0], jnp.zeros_like(tops[0]))
        shown = tops.at[0].set(root)
        result = jnp.concatenate([shown, applied[:, K:]], axis=1).reshape(FROWS, -1)
        return (result, tops[0, NPIV:])
    lower_result, contrib = lax.map(lower_one, (lower_rhs, lower_vectors, lower_factors, merge_vectors, merge_factors, live_blocks))
    target = front_owner[parent_front[:, 0]]
    assembled = upper_rhs.at[target[:, None], contrib_rows].set(contrib)

    def upper_one(operands):
        values, vectors, factors, pair_vectors, pair_factors = operands
        tops, applied = apply_front(values, vectors, factors, pair_vectors, pair_factors, jnp.int32(N_ROWS))
        return jnp.concatenate([tops, applied[:, K:]], axis=1).reshape(FROWS, -1)
    upper_result = lax.map(upper_one, (assembled, upper_vectors, upper_factors, summit_vectors, summit_factors))
    return (lower_result, upper_result)
```

```python
import jax
import jax.numpy as jnp
from jax import lax
from jax.experimental import pallas as pl
from jax.experimental.pallas import tpu as pltpu
from jax.sharding import PartitionSpec as P

N = 512
BR = 1024
K = 256
NPIV = 128
CB = 128
LEVELS = 4
F32 = jnp.float32
BF16 = jnp.bfloat16
HBM = pl.BlockSpec(memory_space=pl.ANY)


TN = ((0,), (0,))
NN = ((1,), (0,))
NT = ((1,), (1,))


def split(x):
    high = x.astype(BF16)
    return high, (x - high.astype(F32)).astype(BF16)


def dot3(a, b, dims):
    def one(p, q):
        return lax.dot_general(p, q, (dims, ((), ())), preferred_element_type=F32)

    return one(a[0], b[0]) + (one(a[0], b[1]) + one(a[1], b[0]))


def full(shape):
    return pl.BlockSpec(shape, lambda *_: (0,) * len(shape))


def spec(shape, index):
    return pl.BlockSpec(shape, lambda *_: index)


def params():
    return pltpu.CompilerParams(vmem_limit_bytes=48 * 1024 * 1024)


def role(info, live_at, level):
    place = info[0]
    step = 1 << level
    at = place % (2 * step)
    live = info[live_at]
    rest = (at == step) & (place < live)
    lead = (at == 0) & (place + step < live)
    return lead, rest


def block_step(info, live_at, front, rhs, vectors, factors, node_vectors, prior, sends, rows=None, data=None, after=()):
    width = N // sends

    def kernel(info, x_ref, y_ref, g_ref, v_ref, *rest):
        out_ref, send_refs = rest[-1 - sends], rest[-sends:]
        x = x_ref[0]
        if rows is not None:
            rows_ref, data_ref = rest[:2]
            slots = lax.broadcasted_iota(jnp.int32, (BR, rows_ref.shape[1]), 0) == rows_ref[0:1, :]
            high, low = split(data_ref[...].reshape(-1, N))
            chosen = jnp.where(slots, 1.0, 0.0)
            taken = jnp.max(chosen, axis=1, keepdims=True) > 0.5
            chosen = chosen.astype(BF16)
            placed = lax.dot_general(chosen, high, (NN, ((), ())), preferred_element_type=F32)
            placed = placed + lax.dot_general(chosen, low, (NN, ((), ())), preferred_element_type=F32)
            x = jnp.where(taken, placed, x)
        active = info[0] < info[live_at]

        @pl.when(active)
        def _():
            y = y_ref[0]
            project = dot3(split(y.T), split(x), NN)
            scaled = dot3(split(g_ref[0].T), split(project), NN)
            out_ref[0] = x - dot3(split(y), split(scaled), NN)

        @pl.when(jnp.logical_not(active))
        def _():
            out_ref[0] = x

        top = out_ref[0, :K]

        @pl.when(info[0] % 2 == 1)
        def _():
            send = dot3(split(v_ref[0].T), split(top), NN)
            for i in range(sends):
                send_refs[i][...] = send[:, i * width : (i + 1) * width]

        @pl.when(info[0] % 2 == 0)
        def _():
            for i in range(sends):
                send_refs[i][...] = top[:, i * width : (i + 1) * width]

    in_specs = [
        spec((1, BR, N), (front, 0, 0)),
        spec((1, BR, K), (front, 0, 0)),
        spec((1, K, K), (front, 0, 0)),
        spec((1, K, K), (front, 0, 0)),
    ]
    operands = [info, rhs, vectors, factors, node_vectors]
    if rows is not None:
        in_specs += [full(rows.shape), full(data.shape)]
        operands += [rows, data]
    aliases = {}
    in_specs += [HBM] * len(after)
    operands += after
    if prior is not None:
        in_specs.append(HBM)
        operands.append(prior)
        aliases = {len(operands) - 1: 0}
    return pl.pallas_call(
        kernel,
        grid_spec=pltpu.PrefetchScalarGridSpec(
            num_scalar_prefetch=1,
            grid=(1,),
            in_specs=in_specs,
            out_specs=[spec((1, BR, N), (front, 0, 0))] + [full((K, width))] * sends,
        ),
        out_shape=[jax.ShapeDtypeStruct(rhs.shape, F32)] + [jax.ShapeDtypeStruct((K, width), F32)] * sends,
        input_output_aliases=aliases,
        compiler_params=params(),
        name=f"block_{live_at}",
    )(*operands)


def tree_level(info, live_at, level, front, top, top_spec, send, recv, node_vectors, node_factors, lead_factors, after=()):
    cols = send.shape[1]
    last = level == LEVELS - 1

    def kernel(info, top_ref, send_ref, recv_ref, v_ref, g_ref, gl_ref, *outs):
        out_ref, *outs = outs[len(after) :]
        lead, rest = role(info, live_at, level)
        top = top_ref[...].reshape(K, cols)

        @pl.when(lead)
        def _():
            inner = send_ref[...] + recv_ref[...]
            out_ref[...] = top - dot3(split(gl_ref[0].T), split(inner), NN)

        @pl.when(rest)
        def _():
            inner = send_ref[...] + recv_ref[...]
            weight = dot3(split(g_ref[0].T), split(inner), NN)
            out_ref[...] = top - dot3(split(v_ref[0]), split(weight), NN)

        @pl.when(jnp.logical_not(lead | rest))
        def _():
            out_ref[...] = top

        if not last:
            at = info[0] % (4 << level)

            @pl.when(at == (2 << level))
            def _():
                outs[0][...] = dot3(split(v_ref[0].T), split(out_ref[...]), NN)

            @pl.when(at == 0)
            def _():
                outs[0][...] = out_ref[...]

    node = spec((1, K, K), (front, 0, 0))
    shape = jax.ShapeDtypeStruct((K, cols), F32)
    flat = full((K, cols))
    count = 1 if last else 2
    outs = pl.pallas_call(
        kernel,
        grid_spec=pltpu.PrefetchScalarGridSpec(
            num_scalar_prefetch=1,
            grid=(1,),
            in_specs=[top_spec, flat, flat, node, node, node] + [HBM] * len(after),
            out_specs=[flat] * count,
        ),
        out_shape=[shape] * count,
        compiler_params=params(),
        name=f"level_{level}",
    )(info, top, send, recv, node_vectors, node_factors, lead_factors, *after)
    return outs


def exchange(value, level):
    return lax.ppermute(value, "rows", [(i, i ^ (1 << level)) for i in range(16)])


def lead_gets(value, level):
    step = 1 << level
    return lax.ppermute(value, "rows", [(b + step, b) for b in range(0, 16, 2 * step)])


def fill_tops(info, applied, front, tops, clear):
    half = N // len(tops)

    def kernel(info, *refs):
        out_ref = refs[-1]
        for i in range(len(tops)):
            out_ref[0, :, i * half : (i + 1) * half] = refs[i][...]
        if clear:

            @pl.when(info[0] == 0)
            def _():
                out_ref[0, NPIV:, :] = jnp.zeros((K - NPIV, N), F32)

    return pl.pallas_call(
        kernel,
        grid_spec=pltpu.PrefetchScalarGridSpec(
            num_scalar_prefetch=1,
            grid=(1,),
            in_specs=[full((K, half))] * len(tops) + [HBM],
            out_specs=spec((1, K, N), (front, 0, 0)),
        ),
        out_shape=jax.ShapeDtypeStruct(applied.shape, F32),
        input_output_aliases={len(tops) + 1: 0},
        compiler_params=params(),
        name="fill_tops",
    )(info, *tops, applied)


def map_node(info, level, lead_in, rest_in, node_vectors, node_factors, after=()):
    fronts = node_vectors.shape[0]
    ins = [] if lead_in is None else [lead_in, rest_in]

    def kernel(info, *refs):
        v_ref, g_ref = refs[len(ins) :][:2]
        lead_out, rest_out = refs[-2:]
        step = 1 << level

        @pl.when(info[0] % (2 * step) == step)
        def _():
            for f in range(fronts):
                if level == LEVELS - 1:
                    row = lax.broadcasted_iota(jnp.int32, (CB, K), 0)
                    col = lax.broadcasted_iota(jnp.int32, (CB, K), 1)
                    whole = jnp.where(col == row + NPIV, 1.0, 0.0)
                else:
                    whole = refs[0][f] + refs[1][f]
                active = info[0] < info[1 + f]

                @pl.when(active)
                def _():
                    scaled = dot3(split(whole), split(g_ref[f]), NT)
                    lead_out[f] = whole - scaled
                    rest_out[f] = -dot3(split(scaled), split(v_ref[f]), NT)

                @pl.when(jnp.logical_not(active))
                def _():
                    lead_out[f] = whole
                    rest_out[f] = jnp.zeros((CB, K), F32)

    shape = jax.ShapeDtypeStruct((fronts, CB, K), F32)
    return pl.pallas_call(
        kernel,
        grid_spec=pltpu.PrefetchScalarGridSpec(
            num_scalar_prefetch=1,
            grid=(1,),
            in_specs=[full((fronts, CB, K))] * len(ins) + [full((fronts, K, K))] * 2 + [HBM] * len(after),
            out_specs=[full((fronts, CB, K))] * 2,
        ),
        out_shape=[shape, shape],
        compiler_params=params(),
        name=f"map_{level}",
    )(info, *ins, node_vectors, node_factors, *after)


def map_rows(info, lead_map, rest_map, applied):
    fronts = applied.shape[0]

    def kernel(info, lead_ref, rest_ref, top_ref, out_ref):
        f = pl.program_id(0)
        odd = info[0] % 2 == 1
        chosen = jnp.where(odd, rest_ref[f], lead_ref[f])
        product = dot3(split(chosen), split(top_ref[0]), NN)
        out_ref[...] = product.reshape(out_ref.shape)

    return pl.pallas_call(
        kernel,
        grid_spec=pltpu.PrefetchScalarGridSpec(
            num_scalar_prefetch=1,
            grid=(fronts,),
            in_specs=[full((fronts, CB, K))] * 2 + [pl.BlockSpec((1, K, N), lambda f, _: (f, 0, 0))],
            out_specs=pl.BlockSpec((16, 1, CB // 16, N), lambda f, _: (0, f, 0, 0)),
        ),
        out_shape=jax.ShapeDtypeStruct((16, fronts, CB // 16, N), F32),
        compiler_params=params(),
        name="map_rows",
    )(info, lead_map, rest_map, applied)


def per_device(
    lower_rhs,
    lower_vectors,
    lower_factors,
    merge_vectors,
    merge_factors,
    live_blocks,
    parent_front,
    front_owner,
    contrib_rows,
    upper_rhs,
    upper_vectors,
    upper_factors,
    summit_vectors,
    summit_factors,
):
    place = lax.axis_index("rows")
    column = lax.axis_index("fronts")
    blocks = lax.axis_size("rows")
    fronts = lower_rhs.shape[0]
    live = lax.dynamic_slice_in_dim(live_blocks, column * fronts, fronts)
    info = jnp.concatenate([jnp.stack([place]), live, jnp.full((1,), blocks, jnp.int32)]).astype(jnp.int32)
    lower_factors, merge_vectors, merge_factors = lower_factors[:, 0], merge_vectors[:, 0], merge_factors[:, 0]
    upper_factors, summit_vectors, summit_factors = upper_factors[:, 0], summit_vectors[:, 0], summit_factors[:, 0]

    share = CB // blocks
    parents = jnp.arange(front_owner.shape[0], dtype=jnp.int32)
    target = jnp.sum(jnp.where(parent_front == parents[None, :], front_owner[None, :], 0), axis=1)
    rows_here = lax.dynamic_slice_in_dim(contrib_rows, place * share, share, 1) - place * BR
    rows_here = jnp.where((target == column)[:, None], rows_here, -1)
    rows_here = jnp.broadcast_to(rows_here.reshape(1, -1), (8, rows_here.size))

    maps = map_node(info, 3, None, None, merge_vectors, merge_factors)
    maps = lax.ppermute(maps[0], "rows", [(8, 4)]), lax.ppermute(maps[1], "rows", [(8, 12)])
    applied, send_a = block_step(info, 1, 0, lower_rhs, lower_vectors, lower_factors, merge_vectors, None, 1)
    maps = map_node(info, 2, *maps, merge_vectors, merge_factors, [send_a])
    maps = (
        lax.ppermute(maps[0], "rows", [(4, 2), (12, 10)]),
        lax.ppermute(maps[1], "rows", [(4, 6), (12, 14)]),
    )
    applied, send_b = block_step(info, 2, 1, lower_rhs, lower_vectors, lower_factors, merge_vectors, applied, 1)
    maps = map_node(info, 1, *maps, merge_vectors, merge_factors, [send_b])
    maps = (
        lax.ppermute(maps[0], "rows", [(i + 2, i + 1) for i in range(0, 16, 4)]),
        lax.ppermute(maps[1], "rows", [(i + 2, i + 3) for i in range(0, 16, 4)]),
    )
    lead_map, rest_map = map_node(info, 0, *maps, merge_vectors, merge_factors)
    lead_map = lax.ppermute(lead_map, "rows", [(i + 1, i) for i in range(0, 16, 2)])

    pieces = map_rows(info, lead_map, rest_map, applied)
    mine = jnp.sum(lax.all_to_all(pieces, "rows", 0, 0), axis=0)
    portions = [lax.all_gather(mine, "fronts", axis=0, tiled=True)]

    lead_factors = [lead_gets(merge_factors, level) for level in range(LEVELS)]
    half = N // 2
    finals = []
    chunks = []
    for f, sends in ((0, [send_a]), (1, [send_b])):
        chunks.append([f, applied, spec((1, K, N), (f, 0, 0)), sends[0]])
    for level in range(LEVELS):
        for c in chunks:
            recv = exchange(c[3], level)
            outs = tree_level(info, 1 + c[0], level, c[0], c[1], c[2], c[3], recv, merge_vectors, merge_factors, lead_factors[level])
            c[1], c[2] = outs[0], full((K, N))
            if level < LEVELS - 1:
                c[3] = outs[1]
    lower_result = fill_tops(info, applied, 0, [chunks[0][1]], True)
    lower_result = fill_tops(info, lower_result, 1, [chunks[1][1]], True)

    lead_factors = [lead_gets(summit_factors, level) for level in range(LEVELS)]
    applied, *sends = block_step(
        info, 3, 0, upper_rhs, upper_vectors, upper_factors, summit_vectors, None, 2, rows_here, portions[0]
    )
    tops = []
    chunks = [[applied, spec((1, K, half), (0, 0, j)), sends[j]] for j in range(2)]
    for level in range(LEVELS):
        for c in chunks:
            recv = exchange(c[2], level)
            outs = tree_level(info, 3, level, 0, c[0], c[1], c[2], recv, summit_vectors, summit_factors, lead_factors[level])
            c[0], c[1] = outs[0], full((K, half))
            if level < LEVELS - 1:
                c[2] = outs[1]
    upper_result = fill_tops(info, applied, 0, [c[0] for c in chunks], False)
    return (lower_result, upper_result)


def solution(mesh):
    placed = (
        P("fronts", "rows", None),
        P("fronts", "rows", None),
        P("fronts", "rows", None, None),
        P("fronts", "rows", None, None),
        P("fronts", "rows", None, None),
        P(),
        P(),
        P(),
        P(),
        P("fronts", "rows", None),
        P("fronts", "rows", None),
        P("fronts", "rows", None, None),
        P("fronts", "rows", None, None),
        P("fronts", "rows", None, None),
    )
    return jax.shard_map(
        per_device,
        mesh=mesh,
        in_specs=placed,
        out_specs=(P("fronts", "rows", None), P("fronts", "rows", None)),
        check_vma=False,
    )
```

```python
import jax
import jax.numpy as jnp
from jax import lax
from jax.experimental import pallas as pl
from jax.experimental.pallas import tpu as pltpu
from jax.sharding import PartitionSpec as P


N = 512
BR = 1024
K = 256
NPIV = 128
CB = 128
LEVELS = 4
F32 = jnp.float32
BF16 = jnp.bfloat16
HBM = pl.BlockSpec(memory_space=pl.ANY)


NN = ((1,), (0,))
NT = ((1,), (1,))


def split(x):
    high = x.astype(BF16)
    return high, (x - high.astype(F32)).astype(BF16)


def dot3(a, b, dims):
    def one(p, q):
        return lax.dot_general(p, q, (dims, ((), ())), preferred_element_type=F32)

    return one(a[0], b[0]) + (one(a[0], b[1]) + one(a[1], b[0]))


def full(shape):
    return pl.BlockSpec(shape, lambda *_: (0,) * len(shape))


def spec(shape, index):
    return pl.BlockSpec(shape, lambda *_: index)


def params():
    return pltpu.CompilerParams(vmem_limit_bytes=48 * 1024 * 1024)


def role(info, live_at, level):
    place = info[0]
    step = 1 << level
    at = place % (2 * step)
    live = info[live_at]
    rest = (at == step) & (place < live)
    lead = (at == 0) & (place + step < live)
    return lead, rest


def block_step(info, live_at, front, rhs, vectors, factors, prior, after=()):
    def kernel(info, x_ref, y_ref, g_ref, *rest):
        out_ref, top_ref = rest[-2:]
        active = info[0] < info[live_at]

        @pl.when(active)
        def _():
            x, y = x_ref[0], y_ref[0]
            project = dot3(split(y.T), split(x), NN)
            scaled = dot3(split(g_ref[0].T), split(project), NN)
            out_ref[0] = x - dot3(split(y), split(scaled), NN)

        @pl.when(jnp.logical_not(active))
        def _():
            out_ref[0] = x_ref[0]

        top_ref[...] = out_ref[0, :K]

    operands = [info, rhs, vectors, factors, *after] + ([] if prior is None else [prior])
    return pl.pallas_call(
        kernel,
        grid_spec=pltpu.PrefetchScalarGridSpec(
            num_scalar_prefetch=1,
            grid=(1,),
            in_specs=[
                spec((1, BR, N), (front, 0, 0)),
                spec((1, BR, K), (front, 0, 0)),
                spec((1, K, K), (front, 0, 0)),
            ]
            + [HBM] * (len(operands) - 4),
            out_specs=[spec((1, BR, N), (front, 0, 0)), full((K, N))],
        ),
        out_shape=[jax.ShapeDtypeStruct(rhs.shape, F32), jax.ShapeDtypeStruct((K, N), F32)],
        input_output_aliases={} if prior is None else {len(operands) - 1: 0},
        compiler_params=params(),
    )(*operands)


def parent_before(info, rhs, vectors, factors, node_vectors, rows, after=()):
    def kernel(info, x_ref, y_ref, g_ref, v_ref, rows_ref, *rest):
        out_ref, unit_ref, send_ref, wide = rest[-4:]
        chosen = lax.broadcasted_iota(jnp.int32, (BR, CB), 0) == rows_ref[0:1, :]
        chosen = jnp.where(chosen, 1.0, 0.0)
        taken = jnp.max(chosen, axis=1, keepdims=True) > 0.5
        wide[:, :N] = jnp.where(taken, 0.0, x_ref[0])
        wide[:, N:] = chosen
        y = y_ref[0]
        project = dot3(split(y.T), split(wide[...]), NN)
        scaled = dot3(split(g_ref[0].T), split(project), NN)
        wide[...] = wide[...] - dot3(split(y), split(scaled), NN)
        out_ref[0] = wide[:, :N]
        unit_ref[...] = wide[:, N:]

        @pl.when(info[0] % 2 == 1)
        def _():
            send_ref[...] = dot3(split(v_ref[0].T), split(wide[:K]), NN)

        @pl.when(info[0] % 2 == 0)
        def _():
            send_ref[...] = wide[:K]

    return pl.pallas_call(
        kernel,
        grid_spec=pltpu.PrefetchScalarGridSpec(
            num_scalar_prefetch=1,
            grid=(1,),
            in_specs=[full((1, BR, N)), full((1, BR, K)), full((1, K, K)), full((1, K, K)), full(rows.shape)]
            + [HBM] * len(after),
            out_specs=[full((1, BR, N)), full((BR, CB)), full((K, N + CB))],
            scratch_shapes=[pltpu.VMEM((BR, N + CB), F32)],
        ),
        out_shape=[
            jax.ShapeDtypeStruct(rhs.shape, F32),
            jax.ShapeDtypeStruct((BR, CB), F32),
            jax.ShapeDtypeStruct((K, N + CB), F32),
        ],
        compiler_params=params(),
        name="parent_before",
    )(info, rhs, vectors, factors, node_vectors, rows, *after)


def parent_after(upper, unit, send, portion, after=()):
    half = N // 2

    def kernel(x_ref, unit_ref, send_ref, data_ref, *rest):
        out_ref, send0, send1 = rest[-3:]
        data = split(data_ref[...].reshape(CB, N))
        sent = send_ref[:, :N] + dot3(split(send_ref[:, N:]), data, NN)
        send0[...] = sent[:, :half]
        send1[...] = sent[:, half:]
        out_ref[0] = x_ref[0] + dot3(split(unit_ref[...]), data, NN)

    out = jax.ShapeDtypeStruct((K, half), F32)
    return pl.pallas_call(
        kernel,
        grid=(1,),
        in_specs=[full(upper.shape), full(unit.shape), full(send.shape), full(portion.shape)] + [HBM] * len(after),
        out_specs=[full(upper.shape), full(out.shape), full(out.shape)],
        out_shape=[jax.ShapeDtypeStruct(upper.shape, F32), out, out],
        input_output_aliases={0: 0},
        compiler_params=params(),
        name="parent_after",
    )(upper, unit, send, portion, *after)


def tree_level(info, live_at, level, front, top, top_spec, send, recv, node_vectors, node_factors, lead_factors, after=()):
    cols = send.shape[1]
    last = level == LEVELS - 1

    def kernel(info, top_ref, send_ref, recv_ref, v_ref, g_ref, gl_ref, *outs):
        out_ref, *outs = outs[len(after) :]
        lead, rest = role(info, live_at, level)
        top = top_ref[...].reshape(K, cols)

        @pl.when(lead)
        def _():
            inner = send_ref[...] + recv_ref[...]
            out_ref[...] = top - dot3(split(gl_ref[0].T), split(inner), NN)

        @pl.when(rest)
        def _():
            inner = send_ref[...] + recv_ref[...]
            weight = dot3(split(g_ref[0].T), split(inner), NN)
            out_ref[...] = top - dot3(split(v_ref[0]), split(weight), NN)

        @pl.when(jnp.logical_not(lead | rest))
        def _():
            out_ref[...] = top

        if not last:
            at = info[0] % (4 << level)

            @pl.when(at == (2 << level))
            def _():
                outs[0][...] = dot3(split(v_ref[0].T), split(out_ref[...]), NN)

            @pl.when(at == 0)
            def _():
                outs[0][...] = out_ref[...]

    node = spec((1, K, K), (front, 0, 0))
    shape = jax.ShapeDtypeStruct((K, cols), F32)
    flat = full((K, cols))
    count = 1 if last else 2
    outs = pl.pallas_call(
        kernel,
        grid_spec=pltpu.PrefetchScalarGridSpec(
            num_scalar_prefetch=1,
            grid=(1,),
            in_specs=[top_spec, flat, flat, node, node, node] + [HBM] * len(after),
            out_specs=[flat] * count,
        ),
        out_shape=[shape] * count,
        compiler_params=params(),
    )(info, top, send, recv, node_vectors, node_factors, lead_factors, *after)
    return outs


def exchange(value, level):
    return lax.ppermute(value, "rows", [(i, i ^ (1 << level)) for i in range(16)])


def lead_gets(value, level):
    step = 1 << level
    return lax.ppermute(value, "rows", [(b + step, b) for b in range(0, 16, 2 * step)])


def node_level(info, live_at, level, front, applied, lead, rest, node_vectors, node_factors, after=()):
    last = level == LEVELS - 1
    height = NPIV if last else K
    rests = [] if rest is None else [rest]

    def kernel(info, _, v_ref, g_ref, lead_ref, *refs):
        out_ref, lead_out, v, g, lead, moved, kept, sems = refs[-8:]
        rows = out_ref.at[front, pl.ds(0, K)]
        step = 1 << level
        node = info[0] % (2 * step) == step
        active = info[0] < info[live_at]

        @pl.when(node)
        def _():
            ins = [
                pltpu.make_async_copy(refs[0] if rests else rows, moved, sems.at[0]),
                pltpu.make_async_copy(v_ref.at[front], v, sems.at[1]),
                pltpu.make_async_copy(lead_ref, lead, sems.at[2]),
                pltpu.make_async_copy(g_ref.at[front], g, sems.at[3]),
            ]
            for copy in ins:
                copy.start()
            for copy in ins:
                copy.wait()

            @pl.when(active)
            def _():
                inner = lead[...] + dot3(split(v[...].T), split(moved[...]), NN)
                weight = dot3(split(g[...].T), split(inner), NN)
                lead[:height] = lead[:height] - weight[:height]
                kept[...] = moved[...] - dot3(split(v[...]), split(weight), NN)

            @pl.when(jnp.logical_not(active))
            def _():
                kept[...] = moved[...]

            outs = [
                pltpu.make_async_copy(lead.at[pl.ds(0, height)], lead_out, sems.at[4]),
                pltpu.make_async_copy(kept, rows, sems.at[5]),
            ]
            for copy in outs:
                copy.start()
            for copy in outs:
                copy.wait()

        if last:

            @pl.when(info[0] == 0)
            def _():
                kept[NPIV:] = jnp.zeros((K - NPIV, N), F32)
                copy = pltpu.make_async_copy(
                    kept.at[pl.ds(NPIV, K - NPIV)], out_ref.at[front, pl.ds(NPIV, K - NPIV)], sems.at[5]
                )
                copy.start()
                copy.wait()

    square, flat = pltpu.VMEM((K, K), F32), pltpu.VMEM((K, N), F32)
    return pl.pallas_call(
        kernel,
        grid_spec=pltpu.PrefetchScalarGridSpec(
            num_scalar_prefetch=1,
            grid=(1,),
            in_specs=[HBM] * (4 + len(rests) + len(after)),
            out_specs=[HBM, HBM],
            scratch_shapes=[square, square, flat, flat, flat, pltpu.SemaphoreType.DMA((6,))],
        ),
        out_shape=[jax.ShapeDtypeStruct(applied.shape, F32), jax.ShapeDtypeStruct((height, N), F32)],
        input_output_aliases={1: 0},
        compiler_params=params(),
    )(info, applied, node_vectors, node_factors, lead, *rests, *after)


def lead_moves(value, level):
    if level == 0:
        return lax.ppermute(value, "rows", [(i, i + 1) for i in range(0, 16, 2)]), None
    step = 1 << level
    at = [(b, b + step) for b in range(0, 16, 2 * step)]
    return (
        lax.ppermute(value, "rows", [(b + step // 2, p) for b, p in at]),
        lax.ppermute(value, "rows", [(p + step // 2, p) for b, p in at]),
    )


def fill_roots(info, applied, leads):
    def kernel(info, *refs):
        out_ref, sems = refs[-2:]

        @pl.when(info[0] == 0)
        def _():
            copies = [
                pltpu.make_async_copy(refs[f], out_ref.at[f, pl.ds(0, NPIV)], sems.at[f]) for f in range(len(leads))
            ]
            for copy in copies:
                copy.start()
            for copy in copies:
                copy.wait()

    return pl.pallas_call(
        kernel,
        grid_spec=pltpu.PrefetchScalarGridSpec(
            num_scalar_prefetch=1,
            grid=(1,),
            in_specs=[HBM] * (len(leads) + 1),
            out_specs=HBM,
            scratch_shapes=[pltpu.SemaphoreType.DMA((len(leads),))],
        ),
        out_shape=jax.ShapeDtypeStruct(applied.shape, F32),
        input_output_aliases={len(leads) + 1: 0},
        compiler_params=params(),
        name="fill_roots",
    )(info, *leads, applied)


def fill_tops(info, applied, front, tops, clear):
    half = N // len(tops)

    def kernel(info, *refs):
        out_ref = refs[-1]
        for i in range(len(tops)):
            out_ref[0, :, i * half : (i + 1) * half] = refs[i][...]
        if clear:

            @pl.when(info[0] == 0)
            def _():
                out_ref[0, NPIV:, :] = jnp.zeros((K - NPIV, N), F32)

    return pl.pallas_call(
        kernel,
        grid_spec=pltpu.PrefetchScalarGridSpec(
            num_scalar_prefetch=1,
            grid=(1,),
            in_specs=[full((K, half))] * len(tops) + [HBM],
            out_specs=spec((1, K, N), (front, 0, 0)),
        ),
        out_shape=jax.ShapeDtypeStruct(applied.shape, F32),
        input_output_aliases={len(tops) + 1: 0},
        compiler_params=params(),
        name="fill_tops",
    )(info, *tops, applied)


def map_node(info, level, lead_in, rest_in, node_vectors, node_factors, after=()):
    fronts = node_vectors.shape[0]
    ins = [] if lead_in is None else [lead_in, rest_in]

    def kernel(info, *refs):
        v_ref, g_ref = refs[len(ins) :][:2]
        lead_out, rest_out = refs[-2:]
        step = 1 << level

        @pl.when(info[0] % (2 * step) == step)
        def _():
            for f in range(fronts):
                if level == LEVELS - 1:
                    row = lax.broadcasted_iota(jnp.int32, (CB, K), 0)
                    col = lax.broadcasted_iota(jnp.int32, (CB, K), 1)
                    whole = jnp.where(col == row + NPIV, 1.0, 0.0)
                else:
                    whole = refs[0][f] + refs[1][f]
                active = info[0] < info[1 + f]

                @pl.when(active)
                def _():
                    scaled = dot3(split(whole), split(g_ref[f]), NT)
                    lead_out[f] = whole - scaled
                    rest_out[f] = -dot3(split(scaled), split(v_ref[f]), NT)

                @pl.when(jnp.logical_not(active))
                def _():
                    lead_out[f] = whole
                    rest_out[f] = jnp.zeros((CB, K), F32)

    shape = jax.ShapeDtypeStruct((fronts, CB, K), F32)
    return pl.pallas_call(
        kernel,
        grid_spec=pltpu.PrefetchScalarGridSpec(
            num_scalar_prefetch=1,
            grid=(1,),
            in_specs=[full((fronts, CB, K))] * len(ins) + [full((fronts, K, K))] * 2 + [HBM] * len(after),
            out_specs=[full((fronts, CB, K))] * 2,
        ),
        out_shape=[shape, shape],
        compiler_params=params(),
    )(info, *ins, node_vectors, node_factors, *after)


def map_rows(info, lead_map, rest_map, *tops, after=()):
    fronts = len(tops)

    def kernel(info, lead_ref, rest_ref, *refs):
        top_refs, out_ref = refs[:fronts], refs[-1]
        odd = info[0] % 2 == 1
        for f in range(fronts):
            chosen = jnp.where(odd, rest_ref[f], lead_ref[f])
            product = dot3(split(chosen), split(top_refs[f][...]), NN)
            out_ref[:, f] = product.reshape(16, CB // 16, N)

    return pl.pallas_call(
        kernel,
        grid_spec=pltpu.PrefetchScalarGridSpec(
            num_scalar_prefetch=1,
            grid=(1,),
            in_specs=[full((fronts, CB, K))] * 2 + [full((K, N))] * fronts + [HBM] * len(after),
            out_specs=full((16, fronts, CB // 16, N)),
        ),
        out_shape=jax.ShapeDtypeStruct((16, fronts, CB // 16, N), F32),
        compiler_params=params(),
        name="map_rows",
    )(info, lead_map, rest_map, *tops, *after)


def per_device(
    lower_rhs,
    lower_vectors,
    lower_factors,
    merge_vectors,
    merge_factors,
    live_blocks,
    parent_front,
    front_owner,
    contrib_rows,
    upper_rhs,
    upper_vectors,
    upper_factors,
    summit_vectors,
    summit_factors,
):
    place = lax.axis_index("rows")
    column = lax.axis_index("fronts")
    blocks = lax.axis_size("rows")
    fronts = lower_rhs.shape[0]
    live = lax.dynamic_slice_in_dim(live_blocks, column * fronts, fronts)
    info = jnp.concatenate([jnp.stack([place]), live, jnp.full((1,), blocks, jnp.int32)]).astype(jnp.int32)
    lower_factors, merge_vectors, merge_factors = lower_factors[:, 0], merge_vectors[:, 0], merge_factors[:, 0]
    upper_factors, summit_vectors, summit_factors = upper_factors[:, 0], summit_vectors[:, 0], summit_factors[:, 0]

    share = CB // blocks
    parents = jnp.arange(front_owner.shape[0], dtype=jnp.int32)
    target = jnp.sum(jnp.where(parent_front == parents[None, :], front_owner[None, :], 0), axis=1)
    rows_here = lax.dynamic_slice_in_dim(contrib_rows, place * share, share, 1) - place * BR
    rows_here = jnp.where((target == column)[:, None], rows_here, -1)
    rows_here = jnp.broadcast_to(rows_here.reshape(1, -1), (8, rows_here.size))

    nodes = merge_vectors, merge_factors
    blocks_in = lower_rhs, lower_vectors, lower_factors
    lead_factors = [lead_gets(summit_factors, level) for level in range(LEVELS)]
    maps = map_node(info, 3, None, None, *nodes)
    maps = maps_move(maps, [(8, 4)], [(8, 12)])
    maps = map_node(info, 2, *maps, *nodes)
    token = maps[0]
    maps = maps_move(maps, [(4, 2), (12, 10)], [(4, 6), (12, 14)])
    applied, top_a = block_step(info, 1, 0, *blocks_in, None, [token])
    in_a = lead_moves(top_a, 0)
    maps = map_node(info, 1, *maps, *nodes, [top_a])
    token = maps[0]
    at = range(2, 16, 4)
    maps = maps_move(maps, [(i, i - 1) for i in at], [(i, i + 1) for i in at])
    applied, top_b = block_step(info, 2, 1, *blocks_in, applied, [token])
    in_b = lead_moves(top_b, 0)
    maps = map_node(info, 0, *maps, *nodes, [top_b])
    lead_map = lax.ppermute(maps[0], "rows", [(i + 1, i) for i in range(0, 16, 2)])
    applied, lead_a = node_level(info, 1, 0, 0, applied, *in_a, *nodes, [maps[1]])
    in_a = lead_moves(lead_a, 1)

    pieces = map_rows(info, lead_map, maps[1], top_a, top_b, after=[lead_a])
    swapped = lax.all_to_all(pieces, "rows", 0, 0)
    applied, lead_b = node_level(info, 2, 0, 1, applied, *in_b, *nodes, [pieces])
    upper, unit, send = parent_before(
        info, upper_rhs, upper_vectors, upper_factors, summit_vectors, rows_here, [lead_b]
    )
    applied, lead_a = node_level(info, 1, 1, 0, applied, *in_a, *nodes, [unit])
    swapped, lead_a, lead_b = lax.optimization_barrier((swapped, lead_a, lead_b))
    in_b = lead_moves(lead_b, 1)
    in_a = lead_moves(lead_a, 2)
    mine = add_all(swapped)
    portion = lax.all_gather(mine, "fronts", axis=0, tiled=True)

    upper, *sends = parent_after(upper, unit, send, portion, lead_factors)
    half = N // 2
    chunks = [[upper, spec((1, K, half), (0, 0, j)), sends[j]] for j in range(2)]
    lower_steps = list(LOWER_STEPS)
    order = sends[1]
    ins = {"a": in_a, "b": in_b}
    for level in range(LEVELS):
        recvs = [exchange(chunks[j][2], level) for j in range(2)]
        for j in range(2):
            if lower_steps:
                name, at = lower_steps.pop(0)
                f = "ab".index(name)
                applied, order = node_level(info, 1 + f, at, f, applied, *ins[name], *nodes, [order])
                if at < LEVELS - 1:
                    ins[name] = lead_moves(order, at + 1)
                else:
                    ins[name] = lax.ppermute(order, "rows", [(8, 0)])
            c = chunks[j]
            outs = tree_level(
                info, 3, level, 0, c[0], c[1], c[2], recvs[j], summit_vectors, summit_factors, lead_factors[level], [order],
            )
            order = outs[0]
            c[0], c[1] = outs[0], full((K, half))
            if level < LEVELS - 1:
                c[2] = outs[1]
    in_a, in_b = ins["a"], ins["b"]
    upper_result = fill_tops(info, upper, 0, [c[0] for c in chunks], False)
    lower_result = fill_roots(info, applied, [in_a, in_b])
    return (lower_result, upper_result)


def maps_move(maps, lead_pairs, rest_pairs):
    return lax.ppermute(maps[0], "rows", lead_pairs), lax.ppermute(maps[1], "rows", rest_pairs)


def add_all(pieces):
    def kernel(in_ref, out_ref):
        total = in_ref[0]
        for i in range(1, in_ref.shape[0]):
            total = total + in_ref[i]
        out_ref[...] = total

    return pl.pallas_call(kernel, out_shape=jax.ShapeDtypeStruct(pieces.shape[1:], F32), name="add_all")(pieces)


LOWER_STEPS = (("b", 1), ("a", 2), ("b", 2), ("a", 3), ("b", 3))


def solution(mesh):
    placed = (
        P("fronts", "rows", None),
        P("fronts", "rows", None),
        P("fronts", "rows", None, None),
        P("fronts", "rows", None, None),
        P("fronts", "rows", None, None),
        P(),
        P(),
        P(),
        P(),
        P("fronts", "rows", None),
        P("fronts", "rows", None),
        P("fronts", "rows", None, None),
        P("fronts", "rows", None, None),
        P("fronts", "rows", None, None),
    )
    return jax.shard_map(
        lambda *args: per_device(*args),
        mesh=mesh,
        in_specs=placed,
        out_specs=(P("fronts", "rows", None), P("fronts", "rows", None)),
        check_vma=False,
    )
```

```python
import jax
import jax.numpy as jnp
from jax import lax
from jax.experimental import pallas as pl
from jax.experimental.pallas import tpu as pltpu
from jax.sharding import PartitionSpec as P


N = 512
BR = 1024
K = 256
NPIV = 128
CB = 128
LEVELS = 4
F32 = jnp.float32
BF16 = jnp.bfloat16
HBM = pl.BlockSpec(memory_space=pl.ANY)
FAR = pl.BlockSpec(memory_space=pltpu.HBM)


NN = ((1,), (0,))
NT = ((1,), (1,))


def split(x):
    high = x.astype(BF16)
    return high, (x - high.astype(F32)).astype(BF16)


def dot3(a, b, dims):
    def one(p, q):
        return lax.dot_general(p, q, (dims, ((), ())), preferred_element_type=F32)

    return one(a[0], b[0]) + (one(a[0], b[1]) + one(a[1], b[0]))


def full(shape):
    return pl.BlockSpec(shape, lambda *_: (0,) * len(shape))


def spec(shape, index):
    return pl.BlockSpec(shape, lambda *_: index)


def params(mebibytes=48):
    return pltpu.CompilerParams(vmem_limit_bytes=mebibytes * 1024 * 1024)


def role(info, live_at, level):
    place = info[0]
    step = 1 << level
    at = place % (2 * step)
    live = info[live_at]
    rest = (at == step) & (place < live)
    lead = (at == 0) & (place + step < live)
    return lead, rest


def row_copies(source, target, sems, at):
    part = [pl.ds(c * K, K) for c in range(BR // K)]
    return [pltpu.make_async_copy(source.at[p], target.at[p], sems.at[at, c]) for c, p in enumerate(part)]


def start_all(*copies):
    for group in zip(*copies):
        for copy in group:
            copy.start()


def wait_all(copies):
    for copy in copies:
        copy.wait()


def block_step(info, live_at, front, rhs, vectors, factors, prior, after=()):
    def kernel(info, x_hbm, y_hbm, g_hbm, *rest):
        out_hbm, top_hbm, x, y, g, sems = rest[-6:]
        active = info[0] < info[live_at]
        x_in = row_copies(x_hbm.at[front], x, sems, 0)
        y_in = row_copies(y_hbm.at[front], y, sems, 1)
        out = row_copies(x, out_hbm.at[front], sems, 2)
        g_in = pltpu.make_async_copy(g_hbm.at[front], g, sems.at[3, 0])
        top = pltpu.make_async_copy(x.at[pl.ds(0, K)], top_hbm, sems.at[3, 1])
        start_all(y_in, x_in)
        g_in.start()

        @pl.when(active)
        def _():
            project = jnp.zeros((K, N), F32)
            for c in range(BR // K):
                y_in[c].wait()
                x_in[c].wait()
                part = slice(c * K, (c + 1) * K)
                project = project + dot3(split(y[part].T), split(x[part]), NN)
            g_in.wait()
            scaled = split(dot3(split(g[...].T), split(project), NN))
            for c in range(BR // K):
                part = slice(c * K, (c + 1) * K)
                x[part] = x[part] - dot3(split(y[part]), scaled, NN)
                out[c].start()
                if c == 0:
                    top.start()

        @pl.when(jnp.logical_not(active))
        def _():
            wait_all(y_in + x_in + [g_in])
            start_all(out + [top])

        wait_all(out + [top])

    operands = [info, rhs, vectors, factors, *after] + ([] if prior is None else [prior])
    return pl.pallas_call(
        kernel,
        grid_spec=pltpu.PrefetchScalarGridSpec(
            num_scalar_prefetch=1,
            grid=(1,),
            in_specs=[FAR] * 3 + [HBM] * (len(operands) - 4),
            out_specs=[HBM, HBM],
            scratch_shapes=[
                pltpu.VMEM((BR, N), F32),
                pltpu.VMEM((BR, K), F32),
                pltpu.VMEM((K, K), F32),
                pltpu.SemaphoreType.DMA((4, BR // K)),
            ],
        ),
        out_shape=[jax.ShapeDtypeStruct(rhs.shape, F32), jax.ShapeDtypeStruct((K, N), F32)],
        input_output_aliases={} if prior is None else {len(operands) - 1: 0},
        compiler_params=params(60),
    )(*operands)


def parent_before(info, rhs, vectors, factors, node_vectors, rows, after=()):
    def kernel(info, x_hbm, y_hbm, g_hbm, v_hbm, rows_ref, *rest):
        out_hbm, unit_ref, send_ref, x, y, g, v, sems = rest[-8:]
        x_in = row_copies(x_hbm.at[0], x, sems, 0)
        y_in = row_copies(y_hbm.at[0], y, sems, 1)
        out = row_copies(x, out_hbm.at[0], sems, 2)
        g_in = pltpu.make_async_copy(g_hbm.at[0], g, sems.at[3, 0])
        v_in = pltpu.make_async_copy(v_hbm.at[0], v, sems.at[3, 1])
        start_all(y_in, x_in)
        start_all([g_in, v_in])
        project = jnp.zeros((K, N), F32)
        project_unit = jnp.zeros((K, CB), F32)
        for c in range(BR // K):
            part = slice(c * K, (c + 1) * K)
            chosen = lax.broadcasted_iota(jnp.int32, (K, CB), 0) + c * K == rows_ref[0:1, :]
            chosen = jnp.where(chosen, 1.0, 0.0)
            taken = jnp.max(chosen, axis=1, keepdims=True) > 0.5
            unit_ref[part] = chosen
            y_in[c].wait()
            x_in[c].wait()
            x[part] = jnp.where(taken, 0.0, x[part])
            turned = split(y[part].T)
            project = project + dot3(turned, split(x[part]), NN)
            project_unit = project_unit + dot3(turned, split(chosen), NN)
        wait_all([g_in, v_in])
        turned = split(g[...].T)
        scaled = split(dot3(turned, split(project), NN))
        scaled_unit = split(dot3(turned, split(project_unit), NN))
        for c in range(BR // K):
            part = slice(c * K, (c + 1) * K)
            high_low = split(y[part])
            x[part] = x[part] - dot3(high_low, scaled, NN)
            out[c].start()
            unit_ref[part] = unit_ref[part] - dot3(high_low, scaled_unit, NN)

        @pl.when(info[0] % 2 == 1)
        def _():
            turned = split(v[...].T)
            send_ref[:, :N] = dot3(turned, split(x[:K]), NN)
            send_ref[:, N:] = dot3(turned, split(unit_ref[:K]), NN)

        @pl.when(info[0] % 2 == 0)
        def _():
            send_ref[:, :N] = x[:K]
            send_ref[:, N:] = unit_ref[:K]

        wait_all(out)

    return pl.pallas_call(
        kernel,
        grid_spec=pltpu.PrefetchScalarGridSpec(
            num_scalar_prefetch=1,
            grid=(1,),
            in_specs=[FAR] * 4 + [full(rows.shape)] + [HBM] * len(after),
            out_specs=[HBM, full((BR, CB)), full((K, N + CB))],
            scratch_shapes=[
                pltpu.VMEM((BR, N), F32),
                pltpu.VMEM((BR, K), F32),
                pltpu.VMEM((K, K), F32),
                pltpu.VMEM((K, K), F32),
                pltpu.SemaphoreType.DMA((4, BR // K)),
            ],
        ),
        out_shape=[
            jax.ShapeDtypeStruct(rhs.shape, F32),
            jax.ShapeDtypeStruct((BR, CB), F32),
            jax.ShapeDtypeStruct((K, N + CB), F32),
        ],
        compiler_params=params(60),
        name="parent_before",
    )(info, rhs, vectors, factors, node_vectors, rows, *after)


def parent_after(upper, unit, send, portion, after=()):
    half = N // 2

    def kernel(x_ref, unit_ref, send_ref, data_ref, *rest):
        out_ref, send0, send1 = rest[-3:]
        data = split(data_ref[...].reshape(CB, N))
        sent = send_ref[:, :N] + dot3(split(send_ref[:, N:]), data, NN)
        send0[...] = sent[:, :half]
        send1[...] = sent[:, half:]
        out_ref[0] = x_ref[0] + dot3(split(unit_ref[...]), data, NN)

    out = jax.ShapeDtypeStruct((K, half), F32)
    return pl.pallas_call(
        kernel,
        grid=(1,),
        in_specs=[full(upper.shape), full(unit.shape), full(send.shape), full(portion.shape)] + [HBM] * len(after),
        out_specs=[full(upper.shape), full(out.shape), full(out.shape)],
        out_shape=[jax.ShapeDtypeStruct(upper.shape, F32), out, out],
        input_output_aliases={0: 0},
        compiler_params=params(),
        name="parent_after",
    )(upper, unit, send, portion, *after)


def tree_level(info, live_at, level, front, top, top_spec, send, recv, node_vectors, node_factors, lead_factors, after=()):
    cols = send.shape[1]
    last = level == LEVELS - 1

    def kernel(info, top_ref, send_ref, recv_ref, v_ref, g_ref, gl_ref, *outs):
        out_ref, *outs = outs[len(after) :]
        lead, rest = role(info, live_at, level)
        top = top_ref[...].reshape(K, cols)

        @pl.when(lead)
        def _():
            inner = send_ref[...] + recv_ref[...]
            out_ref[...] = top - dot3(split(gl_ref[0].T), split(inner), NN)

        @pl.when(rest)
        def _():
            inner = send_ref[...] + recv_ref[...]
            weight = dot3(split(g_ref[0].T), split(inner), NN)
            out_ref[...] = top - dot3(split(v_ref[0]), split(weight), NN)

        @pl.when(jnp.logical_not(lead | rest))
        def _():
            out_ref[...] = top

        if not last:
            at = info[0] % (4 << level)

            @pl.when(at == (2 << level))
            def _():
                outs[0][...] = dot3(split(v_ref[0].T), split(out_ref[...]), NN)

            @pl.when(at == 0)
            def _():
                outs[0][...] = out_ref[...]

    node = spec((1, K, K), (front, 0, 0))
    shape = jax.ShapeDtypeStruct((K, cols), F32)
    flat = full((K, cols))
    count = 1 if last else 2
    outs = pl.pallas_call(
        kernel,
        grid_spec=pltpu.PrefetchScalarGridSpec(
            num_scalar_prefetch=1,
            grid=(1,),
            in_specs=[top_spec, flat, flat, node, node, node] + [HBM] * len(after),
            out_specs=[flat] * count,
        ),
        out_shape=[shape] * count,
        compiler_params=params(),
    )(info, top, send, recv, node_vectors, node_factors, lead_factors, *after)
    return outs


def exchange(value, level):
    return lax.ppermute(value, "rows", [(i, i ^ (1 << level)) for i in range(16)])


def lead_gets(value, level):
    step = 1 << level
    return lax.ppermute(value, "rows", [(b + step, b) for b in range(0, 16, 2 * step)])


def node_level(info, live_at, level, front, applied, lead, rest, node_vectors, node_factors, after=()):
    last = level == LEVELS - 1
    height = NPIV if last else K
    rests = [] if rest is None else [rest]

    def kernel(info, _, v_ref, g_ref, lead_ref, *refs):
        out_ref, lead_out, v, g, lead, moved, kept, sems = refs[-8:]
        rows = out_ref.at[front, pl.ds(0, K)]
        step = 1 << level
        node = info[0] % (2 * step) == step
        active = info[0] < info[live_at]

        @pl.when(node)
        def _():
            ins = [
                pltpu.make_async_copy(refs[0] if rests else rows, moved, sems.at[0]),
                pltpu.make_async_copy(v_ref.at[front], v, sems.at[1]),
                pltpu.make_async_copy(lead_ref, lead, sems.at[2]),
                pltpu.make_async_copy(g_ref.at[front], g, sems.at[3]),
            ]
            for copy in ins:
                copy.start()
            for copy in ins:
                copy.wait()

            @pl.when(active)
            def _():
                inner = lead[...] + dot3(split(v[...].T), split(moved[...]), NN)
                weight = dot3(split(g[...].T), split(inner), NN)
                lead[:height] = lead[:height] - weight[:height]
                kept[...] = moved[...] - dot3(split(v[...]), split(weight), NN)

            @pl.when(jnp.logical_not(active))
            def _():
                kept[...] = moved[...]

            outs = [
                pltpu.make_async_copy(lead.at[pl.ds(0, height)], lead_out, sems.at[4]),
                pltpu.make_async_copy(kept, rows, sems.at[5]),
            ]
            for copy in outs:
                copy.start()
            for copy in outs:
                copy.wait()

        if last:

            @pl.when(info[0] == 0)
            def _():
                kept[NPIV:] = jnp.zeros((K - NPIV, N), F32)
                copy = pltpu.make_async_copy(
                    kept.at[pl.ds(NPIV, K - NPIV)], out_ref.at[front, pl.ds(NPIV, K - NPIV)], sems.at[5]
                )
                copy.start()
                copy.wait()

    square, flat = pltpu.VMEM((K, K), F32), pltpu.VMEM((K, N), F32)
    return pl.pallas_call(
        kernel,
        grid_spec=pltpu.PrefetchScalarGridSpec(
            num_scalar_prefetch=1,
            grid=(1,),
            in_specs=[HBM] * (4 + len(rests) + len(after)),
            out_specs=[HBM, HBM],
            scratch_shapes=[square, square, flat, flat, flat, pltpu.SemaphoreType.DMA((6,))],
        ),
        out_shape=[jax.ShapeDtypeStruct(applied.shape, F32), jax.ShapeDtypeStruct((height, N), F32)],
        input_output_aliases={1: 0},
        compiler_params=params(),
    )(info, applied, node_vectors, node_factors, lead, *rests, *after)


def lead_moves(value, level):
    if level == 0:
        return lax.ppermute(value, "rows", [(i, i + 1) for i in range(0, 16, 2)]), None
    step = 1 << level
    at = [(b, b + step) for b in range(0, 16, 2 * step)]
    return (
        lax.ppermute(value, "rows", [(b + step // 2, p) for b, p in at]),
        lax.ppermute(value, "rows", [(p + step // 2, p) for b, p in at]),
    )


def fill_roots(info, applied, leads):
    def kernel(info, *refs):
        out_ref, sems = refs[-2:]

        @pl.when(info[0] == 0)
        def _():
            copies = [
                pltpu.make_async_copy(refs[f], out_ref.at[f, pl.ds(0, NPIV)], sems.at[f]) for f in range(len(leads))
            ]
            for copy in copies:
                copy.start()
            for copy in copies:
                copy.wait()

    return pl.pallas_call(
        kernel,
        grid_spec=pltpu.PrefetchScalarGridSpec(
            num_scalar_prefetch=1,
            grid=(1,),
            in_specs=[HBM] * (len(leads) + 1),
            out_specs=HBM,
            scratch_shapes=[pltpu.SemaphoreType.DMA((len(leads),))],
        ),
        out_shape=jax.ShapeDtypeStruct(applied.shape, F32),
        input_output_aliases={len(leads) + 1: 0},
        compiler_params=params(),
        name="fill_roots",
    )(info, *leads, applied)


def fill_tops(info, applied, front, tops, clear):
    half = N // len(tops)

    def kernel(info, *refs):
        out_ref = refs[-1]
        for i in range(len(tops)):
            out_ref[0, :, i * half : (i + 1) * half] = refs[i][...]
        if clear:

            @pl.when(info[0] == 0)
            def _():
                out_ref[0, NPIV:, :] = jnp.zeros((K - NPIV, N), F32)

    return pl.pallas_call(
        kernel,
        grid_spec=pltpu.PrefetchScalarGridSpec(
            num_scalar_prefetch=1,
            grid=(1,),
            in_specs=[full((K, half))] * len(tops) + [HBM],
            out_specs=spec((1, K, N), (front, 0, 0)),
        ),
        out_shape=jax.ShapeDtypeStruct(applied.shape, F32),
        input_output_aliases={len(tops) + 1: 0},
        compiler_params=params(),
        name="fill_tops",
    )(info, *tops, applied)


def map_node(info, level, lead_in, rest_in, node_vectors, node_factors, after=()):
    fronts = node_vectors.shape[0]
    ins = [] if lead_in is None else [lead_in, rest_in]

    def kernel(info, *refs):
        v_ref, g_ref = refs[len(ins) :][:2]
        lead_out, rest_out = refs[-2:]
        step = 1 << level

        @pl.when(info[0] % (2 * step) == step)
        def _():
            for f in range(fronts):
                if level == LEVELS - 1:
                    row = lax.broadcasted_iota(jnp.int32, (CB, K), 0)
                    col = lax.broadcasted_iota(jnp.int32, (CB, K), 1)
                    whole = jnp.where(col == row + NPIV, 1.0, 0.0)
                else:
                    whole = refs[0][f] + refs[1][f]
                active = info[0] < info[1 + f]

                @pl.when(active)
                def _():
                    scaled = dot3(split(whole), split(g_ref[f]), NT)
                    lead_out[f] = whole - scaled
                    rest_out[f] = -dot3(split(scaled), split(v_ref[f]), NT)

                @pl.when(jnp.logical_not(active))
                def _():
                    lead_out[f] = whole
                    rest_out[f] = jnp.zeros((CB, K), F32)

    shape = jax.ShapeDtypeStruct((fronts, CB, K), F32)
    return pl.pallas_call(
        kernel,
        grid_spec=pltpu.PrefetchScalarGridSpec(
            num_scalar_prefetch=1,
            grid=(1,),
            in_specs=[full((fronts, CB, K))] * len(ins) + [full((fronts, K, K))] * 2 + [HBM] * len(after),
            out_specs=[full((fronts, CB, K))] * 2,
        ),
        out_shape=[shape, shape],
        compiler_params=params(),
    )(info, *ins, node_vectors, node_factors, *after)


def map_rows(info, lead_map, rest_map, *tops):
    fronts = len(tops)

    def kernel(info, lead_ref, rest_ref, *refs):
        top_refs, out_ref = refs[:fronts], refs[-1]
        odd = info[0] % 2 == 1

        @pl.when(odd)
        def _():
            for f in range(fronts):
                product = dot3(split(lead_ref[f] + rest_ref[f]), split(top_refs[f][...]), NN)
                out_ref[:, f] = product.reshape(16, CB // 16, N)

        @pl.when(jnp.logical_not(odd))
        def _():
            out_ref[...] = jnp.zeros(out_ref.shape, F32)

    return pl.pallas_call(
        kernel,
        grid_spec=pltpu.PrefetchScalarGridSpec(
            num_scalar_prefetch=1,
            grid=(1,),
            in_specs=[full((fronts, CB, K))] * 2 + [full((K, N))] * fronts,
            out_specs=full((16, fronts, CB // 16, N)),
        ),
        out_shape=jax.ShapeDtypeStruct((16, fronts, CB // 16, N), F32),
        compiler_params=params(),
        name="map_rows",
    )(info, lead_map, rest_map, *tops)


def per_device(
    lower_rhs,
    lower_vectors,
    lower_factors,
    merge_vectors,
    merge_factors,
    live_blocks,
    parent_front,
    front_owner,
    contrib_rows,
    upper_rhs,
    upper_vectors,
    upper_factors,
    summit_vectors,
    summit_factors,
):
    place = lax.axis_index("rows")
    column = lax.axis_index("fronts")
    blocks = lax.axis_size("rows")
    fronts = lower_rhs.shape[0]
    live = lax.dynamic_slice_in_dim(live_blocks, column * fronts, fronts)
    info = jnp.concatenate([jnp.stack([place]), live, jnp.full((1,), blocks, jnp.int32)]).astype(jnp.int32)
    lower_factors, merge_vectors, merge_factors = lower_factors[:, 0], merge_vectors[:, 0], merge_factors[:, 0]
    upper_factors, summit_vectors, summit_factors = upper_factors[:, 0], summit_vectors[:, 0], summit_factors[:, 0]

    share = CB // blocks
    parents = jnp.arange(front_owner.shape[0], dtype=jnp.int32)
    target = jnp.sum(jnp.where(parent_front == parents[None, :], front_owner[None, :], 0), axis=1)
    rows_here = lax.dynamic_slice_in_dim(contrib_rows, place * share, share, 1) - place * BR
    rows_here = jnp.where((target == column)[:, None], rows_here, -1)
    rows_here = jnp.broadcast_to(rows_here.reshape(1, -1), (8, rows_here.size))

    nodes = merge_vectors, merge_factors
    blocks_in = lower_rhs, lower_vectors, lower_factors
    lead_factors = [lead_gets(summit_factors, level) for level in range(LEVELS)]
    maps = map_node(info, 3, None, None, *nodes)
    maps = maps_move(maps, [(8, 4)], [(8, 12)])
    maps = map_node(info, 2, *maps, *nodes)
    token = maps[0]
    maps = maps_move(maps, [(4, 2), (12, 10)], [(4, 6), (12, 14)])
    applied, top_a = block_step(info, 1, 0, *blocks_in, None, [token])
    in_a = lead_moves(top_a, 0)
    applied, top_b = block_step(info, 2, 1, *blocks_in, applied)
    in_b = lead_moves(top_b, 0)
    maps = map_node(info, 1, *maps, *nodes, [top_b])
    token = maps[0]
    at = range(2, 16, 4)
    maps = maps_move(maps, [(i, i - 1) for i in at], [(i, i + 1) for i in at])
    upper, unit, send = parent_before(info, upper_rhs, upper_vectors, upper_factors, summit_vectors, rows_here, [token])
    applied, lead_a = node_level(info, 1, 0, 0, applied, *in_a, *nodes, [unit])
    in_a = lead_moves(lead_a, 1)
    applied, lead_b = node_level(info, 2, 0, 1, applied, *in_b, *nodes, [lead_a])
    in_b = lead_moves(lead_b, 1)

    pieces = map_rows(info, *maps, lead_a, lead_b)
    swapped = lax.all_to_all(pieces, "rows", 0, 0)
    applied, lead_a = node_level(info, 1, 1, 0, applied, *in_a, *nodes, [pieces])
    in_a = lead_moves(lead_a, 2)
    applied, lead_b = node_level(info, 2, 1, 1, applied, *in_b, *nodes)
    in_b = lead_moves(lead_b, 2)
    mine = add_all(swapped)
    portion = lax.all_gather(mine, "fronts", axis=0, tiled=True)

    upper, *sends = parent_after(upper, unit, send, portion, lead_factors)
    half = N // 2
    chunks = [[upper, spec((1, K, half), (0, 0, j)), sends[j]] for j in range(2)]
    order = sends[1]
    ins = {"a": in_a, "b": in_b}
    for level in range(LEVELS):
        recvs = [exchange(chunks[j][2], level) for j in range(2)]
        for j in range(2):
            for name, at in LOWER_STEPS.get((level, j), ()):
                f = "ab".index(name)
                applied, order = node_level(info, 1 + f, at, f, applied, *ins[name], *nodes, [order])
                if at < LEVELS - 1:
                    ins[name] = lead_moves(order, at + 1)
                else:
                    ins[name] = lax.ppermute(order, "rows", [(8, 0)])
            c = chunks[j]
            outs = tree_level(
                info, 3, level, 0, c[0], c[1], c[2], recvs[j], summit_vectors, summit_factors, lead_factors[level], [order],
            )
            order = outs[0]
            c[0], c[1] = outs[0], full((K, half))
            if level < LEVELS - 1:
                c[2] = outs[1]
    in_a, in_b = ins["a"], ins["b"]
    upper_result = fill_tops(info, upper, 0, [c[0] for c in chunks], False)
    lower_result = fill_roots(info, applied, [in_a, in_b])
    return (lower_result, upper_result)


def maps_move(maps, lead_pairs, rest_pairs):
    return lax.ppermute(maps[0], "rows", lead_pairs), lax.ppermute(maps[1], "rows", rest_pairs)


def add_all(pieces):
    def kernel(in_ref, out_ref):
        total = in_ref[0]
        for i in range(1, in_ref.shape[0]):
            total = total + in_ref[i]
        out_ref[...] = total

    return pl.pallas_call(kernel, out_shape=jax.ShapeDtypeStruct(pieces.shape[1:], F32), name="add_all")(pieces)


LOWER_STEPS = {(0, 0): (("a", 2), ("b", 2)), (0, 1): (("a", 3),), (1, 1): (("b", 3),)}


def solution(mesh):
    placed = (
        P("fronts", "rows", None),
        P("fronts", "rows", None),
        P("fronts", "rows", None, None),
        P("fronts", "rows", None, None),
        P("fronts", "rows", None, None),
        P(),
        P(),
        P(),
        P(),
        P("fronts", "rows", None),
        P("fronts", "rows", None),
        P("fronts", "rows", None, None),
        P("fronts", "rows", None, None),
        P("fronts", "rows", None, None),
    )
    return jax.shard_map(
        lambda *args: per_device(*args),
        mesh=mesh,
        in_specs=placed,
        out_specs=(P("fronts", "rows", None), P("fronts", "rows", None)),
        check_vma=False,
    )
```

```python
import jax
import jax.numpy as jnp
from jax import lax
from jax.experimental import pallas as pl
from jax.experimental.pallas import tpu as pltpu
from jax.sharding import PartitionSpec as P


N = 512
BR = 1024
K = 256
NPIV = 128
CB = 128
LEVELS = 4
F32 = jnp.float32
BF16 = jnp.bfloat16
HBM = pl.BlockSpec(memory_space=pl.ANY)
FAR = pl.BlockSpec(memory_space=pltpu.HBM)


NN = ((1,), (0,))
NT = ((1,), (1,))


def split(x):
    high = x.astype(BF16)
    return high, (x - high.astype(F32)).astype(BF16)


def dot3(a, b, dims):
    def one(p, q):
        return lax.dot_general(p, q, (dims, ((), ())), preferred_element_type=F32)

    return one(a[0], b[0]) + (one(a[0], b[1]) + one(a[1], b[0]))


def full(shape):
    return pl.BlockSpec(shape, lambda *_: (0,) * len(shape))


def spec(shape, index):
    return pl.BlockSpec(shape, lambda *_: index)


def params(mebibytes=48):
    return pltpu.CompilerParams(vmem_limit_bytes=mebibytes * 1024 * 1024)


def role(info, live_at, level):
    place = info[0]
    step = 1 << level
    at = place % (2 * step)
    live = info[live_at]
    rest = (at == step) & (place < live)
    lead = (at == 0) & (place + step < live)
    return lead, rest


def row_copies(source, target, sems, at):
    part = [pl.ds(c * K, K) for c in range(BR // K)]
    return [pltpu.make_async_copy(source.at[p], target.at[p], sems.at[at, c]) for c, p in enumerate(part)]


def start_all(*copies):
    for group in zip(*copies):
        for copy in group:
            copy.start()


def wait_all(copies):
    for copy in copies:
        copy.wait()


def block_step(info, live_at, front, rhs, vectors, factors, prior, after=()):
    def kernel(info, x_hbm, y_hbm, g_hbm, *rest):
        out_hbm, top_hbm, x, y, g, sems = rest[-6:]
        active = info[0] < info[live_at]
        x_in = row_copies(x_hbm.at[front], x, sems, 0)
        y_in = row_copies(y_hbm.at[front], y, sems, 1)
        out = row_copies(x, out_hbm.at[front], sems, 2)
        g_in = pltpu.make_async_copy(g_hbm.at[front], g, sems.at[3, 0])
        top = pltpu.make_async_copy(x.at[pl.ds(0, K)], top_hbm, sems.at[3, 1])
        start_all(y_in, x_in)
        g_in.start()

        @pl.when(active)
        def _():
            project = jnp.zeros((K, N), F32)
            for c in range(BR // K):
                y_in[c].wait()
                x_in[c].wait()
                part = slice(c * K, (c + 1) * K)
                project = project + dot3(split(y[part].T), split(x[part]), NN)
            g_in.wait()
            scaled = split(dot3(split(g[...].T), split(project), NN))
            for c in range(BR // K):
                part = slice(c * K, (c + 1) * K)
                x[part] = x[part] - dot3(split(y[part]), scaled, NN)
                out[c].start()
                if c == 0:
                    top.start()

        @pl.when(jnp.logical_not(active))
        def _():
            wait_all(y_in + x_in + [g_in])
            start_all(out + [top])

        wait_all(out + [top])

    operands = [info, rhs, vectors, factors, *after] + ([] if prior is None else [prior])
    return pl.pallas_call(
        kernel,
        grid_spec=pltpu.PrefetchScalarGridSpec(
            num_scalar_prefetch=1,
            grid=(1,),
            in_specs=[FAR] * 3 + [HBM] * (len(operands) - 4),
            out_specs=[HBM, HBM],
            scratch_shapes=[
                pltpu.VMEM((BR, N), F32),
                pltpu.VMEM((BR, K), F32),
                pltpu.VMEM((K, K), F32),
                pltpu.SemaphoreType.DMA((4, BR // K)),
            ],
        ),
        out_shape=[jax.ShapeDtypeStruct(rhs.shape, F32), jax.ShapeDtypeStruct((K, N), F32)],
        input_output_aliases={} if prior is None else {len(operands) - 1: 0},
        compiler_params=params(60),
    )(*operands)


def parent_before(info, rhs, vectors, factors, node_vectors, rows, after=()):
    def kernel(info, x_hbm, y_hbm, g_hbm, v_hbm, rows_ref, *rest):
        out_hbm, unit_ref, send_ref, x, y, g, v, sems = rest[-8:]
        x_in = row_copies(x_hbm.at[0], x, sems, 0)
        y_in = row_copies(y_hbm.at[0], y, sems, 1)
        out = row_copies(x, out_hbm.at[0], sems, 2)
        g_in = pltpu.make_async_copy(g_hbm.at[0], g, sems.at[3, 0])
        v_in = pltpu.make_async_copy(v_hbm.at[0], v, sems.at[3, 1])
        start_all(y_in, x_in)
        start_all([g_in, v_in])
        project = jnp.zeros((K, N), F32)
        project_unit = jnp.zeros((K, CB), F32)
        for c in range(BR // K):
            part = slice(c * K, (c + 1) * K)
            chosen = lax.broadcasted_iota(jnp.int32, (K, CB), 0) + c * K == rows_ref[0:1, :]
            chosen = jnp.where(chosen, 1.0, 0.0)
            taken = jnp.max(chosen, axis=1, keepdims=True) > 0.5
            unit_ref[part] = chosen
            y_in[c].wait()
            x_in[c].wait()
            x[part] = jnp.where(taken, 0.0, x[part])
            turned = split(y[part].T)
            project = project + dot3(turned, split(x[part]), NN)
            project_unit = project_unit + dot3(turned, split(chosen), NN)
        wait_all([g_in, v_in])
        turned = split(g[...].T)
        scaled = split(dot3(turned, split(project), NN))
        scaled_unit = split(dot3(turned, split(project_unit), NN))
        for c in range(BR // K):
            part = slice(c * K, (c + 1) * K)
            high_low = split(y[part])
            x[part] = x[part] - dot3(high_low, scaled, NN)
            out[c].start()
            unit_ref[part] = unit_ref[part] - dot3(high_low, scaled_unit, NN)

        @pl.when(info[0] % 2 == 1)
        def _():
            turned = split(v[...].T)
            send_ref[:, :N] = dot3(turned, split(x[:K]), NN)
            send_ref[:, N:] = dot3(turned, split(unit_ref[:K]), NN)

        @pl.when(info[0] % 2 == 0)
        def _():
            send_ref[:, :N] = x[:K]
            send_ref[:, N:] = unit_ref[:K]

        wait_all(out)

    return pl.pallas_call(
        kernel,
        grid_spec=pltpu.PrefetchScalarGridSpec(
            num_scalar_prefetch=1,
            grid=(1,),
            in_specs=[FAR] * 4 + [full(rows.shape)] + [HBM] * len(after),
            out_specs=[HBM, full((BR, CB)), full((K, N + CB))],
            scratch_shapes=[
                pltpu.VMEM((BR, N), F32),
                pltpu.VMEM((BR, K), F32),
                pltpu.VMEM((K, K), F32),
                pltpu.VMEM((K, K), F32),
                pltpu.SemaphoreType.DMA((4, BR // K)),
            ],
        ),
        out_shape=[
            jax.ShapeDtypeStruct(rhs.shape, F32),
            jax.ShapeDtypeStruct((BR, CB), F32),
            jax.ShapeDtypeStruct((K, N + CB), F32),
        ],
        compiler_params=params(60),
        name="parent_before",
    )(info, rhs, vectors, factors, node_vectors, rows, *after)


def parent_after(upper, unit, send, portion, after=()):
    half = N // 2

    def kernel(x_ref, unit_ref, send_ref, data_ref, *rest):
        out_ref, send0, send1 = rest[-3:]
        data = split(data_ref[...].reshape(CB, N))
        sent = send_ref[:, :N] + dot3(split(send_ref[:, N:]), data, NN)
        send0[...] = sent[:, :half]
        send1[...] = sent[:, half:]
        out_ref[0] = x_ref[0] + dot3(split(unit_ref[...]), data, NN)

    out = jax.ShapeDtypeStruct((K, half), F32)
    return pl.pallas_call(
        kernel,
        grid=(1,),
        in_specs=[full(upper.shape), full(unit.shape), full(send.shape), full(portion.shape)] + [HBM] * len(after),
        out_specs=[full(upper.shape), full(out.shape), full(out.shape)],
        out_shape=[jax.ShapeDtypeStruct(upper.shape, F32), out, out],
        input_output_aliases={0: 0},
        compiler_params=params(),
        name="parent_after",
    )(upper, unit, send, portion, *after)


def tree_level(info, live_at, level, front, top, top_spec, send, recv, node_vectors, node_factors, lead_factors, after=(), into=None, half=0):
    cols = send.shape[1]
    last = level == LEVELS - 1
    extra = [*after] if into is None else [*after, into]

    def kernel(info, top_ref, send_ref, recv_ref, v_ref, g_ref, gl_ref, *outs):
        out_ref, *outs = outs[len(extra) :]
        lead, rest = role(info, live_at, level)
        top = top_ref[...].reshape(K, cols)

        @pl.when(lead)
        def _():
            inner = send_ref[...] + recv_ref[...]
            out_ref[...] = (top - dot3(split(gl_ref[0].T), split(inner), NN)).reshape(out_ref.shape)

        @pl.when(rest)
        def _():
            inner = send_ref[...] + recv_ref[...]
            weight = dot3(split(g_ref[0].T), split(inner), NN)
            out_ref[...] = (top - dot3(split(v_ref[0]), split(weight), NN)).reshape(out_ref.shape)

        @pl.when(jnp.logical_not(lead | rest))
        def _():
            out_ref[...] = top.reshape(out_ref.shape)

        if not last:
            at = info[0] % (4 << level)

            @pl.when(at == (2 << level))
            def _():
                outs[0][...] = dot3(split(v_ref[0].T), split(out_ref[...]), NN)

            @pl.when(at == 0)
            def _():
                outs[0][...] = out_ref[...]

    node = spec((1, K, K), (front, 0, 0))
    shape = jax.ShapeDtypeStruct((K, cols), F32)
    flat = full((K, cols))
    count = 1 if last else 2
    outs = pl.pallas_call(
        kernel,
        grid_spec=pltpu.PrefetchScalarGridSpec(
            num_scalar_prefetch=1,
            grid=(1,),
            in_specs=[top_spec, flat, flat, node, node, node] + [HBM] * len(extra),
            out_specs=[flat] * count if into is None else [spec((1, K, cols), (0, 0, half))],
        ),
        out_shape=[shape] * count if into is None else [jax.ShapeDtypeStruct(into.shape, F32)],
        input_output_aliases={} if into is None else {6 + len(extra): 0},
        compiler_params=params(),
    )(info, top, send, recv, node_vectors, node_factors, lead_factors, *extra)
    return outs


def exchange(value, level):
    return lax.ppermute(value, "rows", [(i, i ^ (1 << level)) for i in range(16)])


def lead_gets(value, level):
    step = 1 << level
    return lax.ppermute(value, "rows", [(b + step, b) for b in range(0, 16, 2 * step)])


def node_level(info, live_at, level, front, applied, lead, rest, node_vectors, node_factors, after=()):
    last = level == LEVELS - 1
    height = NPIV if last else K
    rests = [] if rest is None else [rest]

    def kernel(info, _, v_ref, g_ref, lead_ref, *refs):
        out_ref, lead_out, v, g, lead, moved, kept, sems = refs[-8:]
        rows = out_ref.at[front, pl.ds(0, K)]
        step = 1 << level
        node = info[0] % (2 * step) == step
        active = info[0] < info[live_at]

        @pl.when(node)
        def _():
            ins = [
                pltpu.make_async_copy(refs[0] if rests else rows, moved, sems.at[0]),
                pltpu.make_async_copy(v_ref.at[front], v, sems.at[1]),
                pltpu.make_async_copy(lead_ref, lead, sems.at[2]),
                pltpu.make_async_copy(g_ref.at[front], g, sems.at[3]),
            ]
            for copy in ins:
                copy.start()
            for copy in ins:
                copy.wait()

            @pl.when(active)
            def _():
                inner = lead[...] + dot3(split(v[...].T), split(moved[...]), NN)
                weight = dot3(split(g[...].T), split(inner), NN)
                lead[:height] = lead[:height] - weight[:height]
                kept[...] = moved[...] - dot3(split(v[...]), split(weight), NN)

            @pl.when(jnp.logical_not(active))
            def _():
                kept[...] = moved[...]

            outs = [
                pltpu.make_async_copy(lead.at[pl.ds(0, height)], lead_out, sems.at[4]),
                pltpu.make_async_copy(kept, rows, sems.at[5]),
            ]
            for copy in outs:
                copy.start()
            for copy in outs:
                copy.wait()

        if last:

            @pl.when(info[0] == 0)
            def _():
                kept[NPIV:] = jnp.zeros((K - NPIV, N), F32)
                copy = pltpu.make_async_copy(
                    kept.at[pl.ds(NPIV, K - NPIV)], out_ref.at[front, pl.ds(NPIV, K - NPIV)], sems.at[5]
                )
                copy.start()
                copy.wait()

    square, flat = pltpu.VMEM((K, K), F32), pltpu.VMEM((K, N), F32)
    return pl.pallas_call(
        kernel,
        grid_spec=pltpu.PrefetchScalarGridSpec(
            num_scalar_prefetch=1,
            grid=(1,),
            in_specs=[HBM] * (4 + len(rests) + len(after)),
            out_specs=[HBM, HBM],
            scratch_shapes=[square, square, flat, flat, flat, pltpu.SemaphoreType.DMA((6,))],
        ),
        out_shape=[jax.ShapeDtypeStruct(applied.shape, F32), jax.ShapeDtypeStruct((height, N), F32)],
        input_output_aliases={1: 0},
        compiler_params=params(),
    )(info, applied, node_vectors, node_factors, lead, *rests, *after)


def lead_moves(value, level):
    if level == 0:
        return lax.ppermute(value, "rows", [(i, i + 1) for i in range(0, 16, 2)]), None
    step = 1 << level
    at = [(b, b + step) for b in range(0, 16, 2 * step)]
    return (
        lax.ppermute(value, "rows", [(b + step // 2, p) for b, p in at]),
        lax.ppermute(value, "rows", [(p + step // 2, p) for b, p in at]),
    )


def fill_roots(info, applied, leads):
    def kernel(info, *refs):
        out_ref, sems = refs[-2:]

        @pl.when(info[0] == 0)
        def _():
            copies = [
                pltpu.make_async_copy(refs[f], out_ref.at[f, pl.ds(0, NPIV)], sems.at[f]) for f in range(len(leads))
            ]
            for copy in copies:
                copy.start()
            for copy in copies:
                copy.wait()

    return pl.pallas_call(
        kernel,
        grid_spec=pltpu.PrefetchScalarGridSpec(
            num_scalar_prefetch=1,
            grid=(1,),
            in_specs=[HBM] * (len(leads) + 1),
            out_specs=HBM,
            scratch_shapes=[pltpu.SemaphoreType.DMA((len(leads),))],
        ),
        out_shape=jax.ShapeDtypeStruct(applied.shape, F32),
        input_output_aliases={len(leads) + 1: 0},
        compiler_params=params(),
        name="fill_roots",
    )(info, *leads, applied)


def map_node(info, level, lead_in, rest_in, node_vectors, node_factors, after=()):
    fronts = node_vectors.shape[0]
    ins = [] if lead_in is None else [lead_in, rest_in]

    def kernel(info, *refs):
        v_ref, g_ref = refs[len(ins) :][:2]
        lead_out, rest_out = refs[-2:]
        step = 1 << level

        @pl.when(info[0] % (2 * step) == step)
        def _():
            for f in range(fronts):
                if level == LEVELS - 1:
                    row = lax.broadcasted_iota(jnp.int32, (CB, K), 0)
                    col = lax.broadcasted_iota(jnp.int32, (CB, K), 1)
                    whole = jnp.where(col == row + NPIV, 1.0, 0.0)
                else:
                    whole = refs[0][f] + refs[1][f]
                active = info[0] < info[1 + f]

                @pl.when(active)
                def _():
                    scaled = dot3(split(whole), split(g_ref[f]), NT)
                    lead_out[f] = whole - scaled
                    rest_out[f] = -dot3(split(scaled), split(v_ref[f]), NT)

                @pl.when(jnp.logical_not(active))
                def _():
                    lead_out[f] = whole
                    rest_out[f] = jnp.zeros((CB, K), F32)

    shape = jax.ShapeDtypeStruct((fronts, CB, K), F32)
    return pl.pallas_call(
        kernel,
        grid_spec=pltpu.PrefetchScalarGridSpec(
            num_scalar_prefetch=1,
            grid=(1,),
            in_specs=[full((fronts, CB, K))] * len(ins) + [full((fronts, K, K))] * 2 + [HBM] * len(after),
            out_specs=[full((fronts, CB, K))] * 2,
        ),
        out_shape=[shape, shape],
        compiler_params=params(),
    )(info, *ins, node_vectors, node_factors, *after)


def map_rows(info, lead_map, rest_map, *tops):
    fronts = len(tops)

    def kernel(info, lead_ref, rest_ref, *refs):
        top_refs, out_ref = refs[:fronts], refs[-1]
        odd = info[0] % 2 == 1

        @pl.when(odd)
        def _():
            for f in range(fronts):
                product = dot3(split(lead_ref[f] + rest_ref[f]), split(top_refs[f][...]), NN)
                out_ref[:, f] = product.reshape(16, CB // 16, N)

        @pl.when(jnp.logical_not(odd))
        def _():
            out_ref[...] = jnp.zeros(out_ref.shape, F32)

    return pl.pallas_call(
        kernel,
        grid_spec=pltpu.PrefetchScalarGridSpec(
            num_scalar_prefetch=1,
            grid=(1,),
            in_specs=[full((fronts, CB, K))] * 2 + [full((K, N))] * fronts,
            out_specs=full((16, fronts, CB // 16, N)),
        ),
        out_shape=jax.ShapeDtypeStruct((16, fronts, CB // 16, N), F32),
        compiler_params=params(),
        name="map_rows",
    )(info, lead_map, rest_map, *tops)


def per_device(
    lower_rhs,
    lower_vectors,
    lower_factors,
    merge_vectors,
    merge_factors,
    live_blocks,
    parent_front,
    front_owner,
    contrib_rows,
    upper_rhs,
    upper_vectors,
    upper_factors,
    summit_vectors,
    summit_factors,
):
    place = lax.axis_index("rows")
    column = lax.axis_index("fronts")
    blocks = lax.axis_size("rows")
    fronts = lower_rhs.shape[0]
    live = lax.dynamic_slice_in_dim(live_blocks, column * fronts, fronts)
    info = jnp.concatenate([jnp.stack([place]), live, jnp.full((1,), blocks, jnp.int32)]).astype(jnp.int32)
    lower_factors, merge_vectors, merge_factors = lower_factors[:, 0], merge_vectors[:, 0], merge_factors[:, 0]
    upper_factors, summit_vectors, summit_factors = upper_factors[:, 0], summit_vectors[:, 0], summit_factors[:, 0]

    share = CB // blocks
    parents = jnp.arange(front_owner.shape[0], dtype=jnp.int32)
    target = jnp.sum(jnp.where(parent_front == parents[None, :], front_owner[None, :], 0), axis=1)
    rows_here = lax.dynamic_slice_in_dim(contrib_rows, place * share, share, 1) - place * BR
    rows_here = jnp.where((target == column)[:, None], rows_here, -1)
    rows_here = jnp.broadcast_to(rows_here.reshape(1, -1), (8, rows_here.size))

    nodes = merge_vectors, merge_factors
    blocks_in = lower_rhs, lower_vectors, lower_factors
    lead_factors = [lead_gets(summit_factors, level) for level in range(LEVELS)]
    maps = map_node(info, 3, None, None, *nodes)
    maps = maps_move(maps, [(8, 4)], [(8, 12)])
    maps = map_node(info, 2, *maps, *nodes)
    token = maps[0]
    maps = maps_move(maps, [(4, 2), (12, 10)], [(4, 6), (12, 14)])
    applied, top_a = block_step(info, 1, 0, *blocks_in, None, [token])
    in_a = lead_moves(top_a, 0)
    applied, top_b = block_step(info, 2, 1, *blocks_in, applied)
    in_b = lead_moves(top_b, 0)
    maps = map_node(info, 1, *maps, *nodes, [top_b])
    token = maps[0]
    at = range(2, 16, 4)
    maps = maps_move(maps, [(i, i - 1) for i in at], [(i, i + 1) for i in at])
    upper, unit, send = parent_before(info, upper_rhs, upper_vectors, upper_factors, summit_vectors, rows_here, [token])
    applied, lead_a = node_level(info, 1, 0, 0, applied, *in_a, *nodes, [unit])
    in_a = lead_moves(lead_a, 1)
    applied, lead_b = node_level(info, 2, 0, 1, applied, *in_b, *nodes, [lead_a])
    in_b = lead_moves(lead_b, 1)

    pieces = map_rows(info, *maps, lead_a, lead_b)
    swapped = lax.all_to_all(pieces, "rows", 0, 0)
    applied, lead_a = node_level(info, 1, 1, 0, applied, *in_a, *nodes, [pieces])
    in_a = lead_moves(lead_a, 2)
    applied, lead_b = node_level(info, 2, 1, 1, applied, *in_b, *nodes)
    in_b = lead_moves(lead_b, 2)
    mine = add_all(swapped)
    portion = lax.all_gather(mine, "fronts", axis=0, tiled=True)

    upper, *sends = parent_after(upper, unit, send, portion, lead_factors)
    half = N // 2
    chunks = [[upper, spec((1, K, half), (0, 0, j)), sends[j]] for j in range(2)]
    order = sends[1]
    ins = {"a": in_a, "b": in_b}
    for level in range(LEVELS):
        recvs = [exchange(chunks[j][2], level) for j in range(2)]
        for j in range(2):
            for name, at in LOWER_STEPS.get((level, j), ()):
                f = "ab".index(name)
                applied, order = node_level(info, 1 + f, at, f, applied, *ins[name], *nodes, [order])
                if at < LEVELS - 1:
                    ins[name] = lead_moves(order, at + 1)
                else:
                    ins[name] = lax.ppermute(order, "rows", [(8, 0)])
            c = chunks[j]
            outs = tree_level(
                info, 3, level, 0, c[0], c[1], c[2], recvs[j], summit_vectors, summit_factors, lead_factors[level], [order],
                upper if level == LEVELS - 1 else None, j,
            )
            if level == LEVELS - 1:
                upper = outs[0]
            order = outs[0]
            c[0], c[1] = outs[0], full((K, half))
            if level < LEVELS - 1:
                c[2] = outs[1]
    in_a, in_b = ins["a"], ins["b"]
    upper_result = upper
    lower_result = fill_roots(info, applied, [in_a, in_b])
    return (lower_result, upper_result)


def maps_move(maps, lead_pairs, rest_pairs):
    return lax.ppermute(maps[0], "rows", lead_pairs), lax.ppermute(maps[1], "rows", rest_pairs)


def add_all(pieces):
    def kernel(in_ref, out_ref):
        total = in_ref[0]
        for i in range(1, in_ref.shape[0]):
            total = total + in_ref[i]
        out_ref[...] = total

    return pl.pallas_call(kernel, out_shape=jax.ShapeDtypeStruct(pieces.shape[1:], F32), name="add_all")(pieces)


LOWER_STEPS = {(0, 0): (("a", 2), ("b", 2)), (0, 1): (("a", 3),), (1, 1): (("b", 3),)}


def solution(mesh):
    placed = (
        P("fronts", "rows", None),
        P("fronts", "rows", None),
        P("fronts", "rows", None, None),
        P("fronts", "rows", None, None),
        P("fronts", "rows", None, None),
        P(),
        P(),
        P(),
        P(),
        P("fronts", "rows", None),
        P("fronts", "rows", None),
        P("fronts", "rows", None, None),
        P("fronts", "rows", None, None),
        P("fronts", "rows", None, None),
    )
    return jax.shard_map(
        lambda *args: per_device(*args),
        mesh=mesh,
        in_specs=placed,
        out_specs=(P("fronts", "rows", None), P("fronts", "rows", None)),
        check_vma=False,
    )
```
